32 devices in a mesh: leaf: 16 (over z, y, x), rows: 2 (over core).
Axes of the slice: x: 2, y: 2, z: 4, core: 2. Of those that a mesh axis runs over, the one named last changes fastest.
Arguments:
- diag_blocks: float32 [16384, 512], P(('leaf', 'rows')), as said below
- rhs: float32 [16384, 512], P(('leaf', 'rows')), may hold values from -9 to 9
- bases: float32 [16384, 384], P(('leaf', 'rows')), may hold values from -0.53033009 to 0.53033009
- coupling_one: float32 [4096, 128], P(('leaf', 'rows')), may hold values from -1 to 1
- coupling_two: float32 [1024, 128], P(('leaf', 'rows')), may hold values from -0.75 to 0.75
- coupling_top: float32 [256, 128], P(('leaf', 'rows')), may hold values from -1 to 1
Outputs:
- solution: float32 [16384, 512], P(('leaf', 'rows'))
The draws below stay inside these ranges and needn't reach their ends.
Inputs may be any that keep to these rules, and one draw needn't show every extreme that they name: `diag_blocks`: every leaf block is symmetric with a diagonal larger than the sum of magnitudes of its row's other entries.
All inputs are finite; a program needn't handle non-finite values.
Results may differ from the reference program's by a relative error of at most 0.00025.
Values sent between devices are 32-bit elements; how exact they have to be, the bound alone decides.
No kernel may reach another device: no remote copies, remote signals or barrier semaphores. Data moves between devices by JAX's collectives and lax.ppermute only.
A program may use at most 64 MiB of HBM per device.

```python
import jax
import jax.numpy as jnp
from jax import lax

LEAF = 512
RANK = 128
NRHS = 512
LEVELS = 3
BLOCKS = 32
ORDER = 16384


def sign_rows(key):
    flips = jax.random.randint(jax.random.fold_in(key, 7), (BLOCKS, LEAF), 0, 2)
    return (2 * flips - 1).astype(jnp.float32)


def draw_diag_blocks(key, part):
    base_key = jax.random.fold_in(key, 11)
    rough_key, margin_key, scale_key, flip_key = jax.random.split(base_key, 4)
    flips = jax.random.randint(flip_key, (BLOCKS, LEAF), 0, 2)
    conj = (2 * flips - 1).astype(jnp.float32)
    rough = jax.random.uniform(rough_key, (BLOCKS, LEAF, LEAF), jnp.float32, 0.5, 1.5)
    margin = jnp.exp(jax.random.uniform(margin_key, (BLOCKS, LEAF), jnp.float32, jnp.log(0.05), jnp.log(1.0)))
    row_scale = jnp.exp(jax.random.uniform(scale_key, (BLOCKS, LEAF), jnp.float32, 0.0, jnp.log(2.0)))
    rough = 0.5 * (rough + jnp.swapaxes(rough, 1, 2))
    place = jnp.arange(LEAF, dtype=jnp.float32)
    distance = jnp.abs(place[:, None] - place[None, :])
    kernel = 1.0 / (1.0 + distance / 4.0) ** 2
    identity = jnp.eye(LEAF, dtype=jnp.float32)
    outer_scale = (conj * row_scale)[:, :, None] * (conj * row_scale)[:, None, :]
    off_part = -(kernel[None, :, :] * rough) * outer_scale * (1.0 - identity)
    row_total = jnp.sum(jnp.abs(off_part), axis=2)
    matrix = off_part + identity * (row_total + margin * row_scale * row_scale)[:, :, None]
    return matrix.reshape(BLOCKS * LEAF, LEAF)


def draw_rhs(key, part):
    noise_key, column_key = jax.random.split(jax.random.fold_in(key, 23))
    signs = sign_rows(key).reshape(BLOCKS * LEAF, 1)
    column_factor = jnp.clip(jax.random.normal(column_key, (NRHS,), jnp.float32), -3.0, 3.0)
    noise = jnp.clip(jax.random.normal(noise_key, (BLOCKS * LEAF, NRHS), jnp.float32), -6.0, 6.0)
    return noise + signs * column_factor[None, :]


def draw_bases(key, part):
    noise_key, column_key = jax.random.split(jax.random.fold_in(key, 37))
    signs = sign_rows(key).reshape(BLOCKS * LEAF, 1)
    column_factor = jnp.clip(jax.random.normal(column_key, (LEVELS * RANK,), jnp.float32), -3.0, 3.0)
    scale_leaf = LEAF ** (-0.5)
    noise = jnp.clip(jax.random.normal(noise_key, (BLOCKS * LEAF, LEVELS * RANK), jnp.float32), -6.0, 6.0) * scale_leaf
    amplitude = 1.6 * scale_leaf
    return noise + amplitude * signs * column_factor[None, :]


def block_levels(own_key, shape, shards, least, high):
    level, own = 1.0, jax.random.fold_in(own_key, 6)
    for axis_at, parts in shards:
        draws = jnp.exp(jax.random.uniform(jax.random.fold_in(own, axis_at), (parts,), jnp.float32, least / len(shards), high / len(shards)))
        level = level * jnp.repeat(draws, shape[axis_at] // parts).reshape([-1 if axis == axis_at else 1 for axis in range(len(shape))])
    return level


def scatter_about(rng, shape, scale, most, shards=(), kind=jnp.bfloat16):
    drawn = jax.random.normal(rng, shape, jnp.float32) * scale
    if len(shards) > 0:
        drawn = block_levels(rng, shape, shards, -0.22, 0.18) * drawn
    return jnp.clip(drawn, min=-most, max=most).astype(kind)


def setup_inputs(seed: int = 0) -> dict:
    seeds = jax.random.split(jax.random.key(seed), 7)
    return {
        "diag_blocks": draw_diag_blocks(jax.random.fold_in(seeds[6], 71), 0),
        "rhs": draw_rhs(jax.random.fold_in(seeds[6], 71), 0),
        "bases": draw_bases(jax.random.fold_in(seeds[6], 71), 0),
        "coupling_one": scatter_about(seeds[3], (BLOCKS * RANK, RANK), (0.8 / RANK ** 0.5), 1.0, ((0, 32),), jnp.float32),
        "coupling_two": scatter_about(seeds[4], (BLOCKS * RANK // 4, RANK), (0.6 / RANK ** 0.5), 0.75, ((0, 32),), jnp.float32),
        "coupling_top": scatter_about(seeds[5], (BLOCKS * RANK // 16, RANK), (0.8 / RANK ** 0.5), 1.0, ((0, 32),), jnp.float32),
    }


def leaf_solve(pieces):
    block, columns = pieces
    lower_factor = jnp.linalg.cholesky(block)
    forward = jax.scipy.linalg.solve_triangular(lower_factor, columns, lower=True)
    return jax.scipy.linalg.solve_triangular(lower_factor.T, forward, lower=False)

def couple(weight_blocks, projected, coupling_blocks):
    highest = lax.Precision.HIGHEST
    inner_term = jnp.einsum('crs,csb->crb', weight_blocks, coupling_blocks, precision=highest)
    system = jnp.eye(RANK, dtype=jnp.float32) + jnp.einsum('cra,crb->ab', coupling_blocks, inner_term, precision=highest)
    right_part = jnp.einsum('cra,crk->ak', coupling_blocks, projected, precision=highest)
    lower_factor = jnp.linalg.cholesky(system)
    coeffs = jax.scipy.linalg.cho_solve((lower_factor, True), right_part)
    return jnp.einsum('crs,sk->crk', coupling_blocks, coeffs, precision=highest)

def reference(diag_blocks, rhs, bases, coupling_one, coupling_two, coupling_top):
    highest = lax.Precision.HIGHEST
    blocks = diag_blocks.reshape(BLOCKS, LEAF, LEAF)
    columns = jnp.concatenate([rhs, bases], 1).reshape(BLOCKS, LEAF, -1)
    solved = lax.map(leaf_solve, (blocks, columns)).reshape(ORDER, -1)
    solution = solved[:, :NRHS]
    basis_solved = [solved[:, NRHS + k * RANK:NRHS + (k + 1) * RANK] for k in range(LEVELS)]
    couplings = [coupling_one, coupling_two, coupling_top]
    for level_index in range(LEVELS):
        node_size = 4 ** level_index
        children = BLOCKS // node_size if level_index == LEVELS - 1 else 4
        groups_count = BLOCKS // (node_size * children)
        node_rows = LEAF * node_size
        remain = jnp.concatenate([solution] + basis_solved[level_index + 1:], 1)
        width_cols = remain.shape[1]
        basis_rows = bases[:, level_index * RANK:(level_index + 1) * RANK].reshape(groups_count, children, node_rows, RANK)
        basis_solve = basis_solved[level_index].reshape(groups_count, children, node_rows, RANK)
        remain_grouped = remain.reshape(groups_count, children, node_rows, width_cols)
        weight_blocks = jnp.einsum('gcnr,gcnk->gcrk', basis_rows, basis_solve, precision=highest)
        projected = jnp.einsum('gcnr,gcnk->gcrk', basis_rows, remain_grouped, precision=highest)
        coupling_mats = couplings[level_index].reshape(groups_count, children, RANK, RANK)
        correction = jax.vmap(couple)(weight_blocks, projected, coupling_mats)
        remain_grouped = remain_grouped - jnp.einsum('gcnr,gcrk->gcnk', basis_solve, correction, precision=highest)
        remain = remain_grouped.reshape(ORDER, width_cols)
        solution = remain[:, :NRHS]
        for later in range(level_index + 1, LEVELS):
            start = NRHS + (later - level_index - 1) * RANK
            basis_solved[later] = remain[:, start:start + RANK]
    return solution
```

```python
import functools

import jax
import jax.numpy as jnp
from jax import lax
from jax.experimental import pallas as pl
from jax.experimental.pallas import tpu as pltpu
from jax.sharding import PartitionSpec as P

AXES = ("leaf", "rows")
F32 = jnp.float32
BF16 = jnp.bfloat16
VMEM = pl.BlockSpec(memory_space=pltpu.VMEM)
FALLBACK_STEPS = 32


def partner(block, flip):
    count = lax.axis_size(AXES)
    return lax.ppermute(block, AXES, [(low, low ^ flip) for low in range(count)])


def split(value):
    high = value.astype(BF16)
    return high, (value - high.astype(F32)).astype(BF16)


def dot1(left, right):
    return jnp.dot(left, right, preferred_element_type=F32)


def dot3(left, right):
    left_high, left_low = split(left)
    right_high, right_low = split(right)
    return dot1(left_high, right_high) + (dot1(left_high, right_low) + dot1(left_low, right_high))


def dot6(left, right):
    return jnp.dot(left, right, preferred_element_type=F32, precision=lax.Precision.HIGHEST)


def eye(order):
    rows = lax.broadcasted_iota(jnp.int32, (order, order), 0)
    cols = lax.broadcasted_iota(jnp.int32, (order, order), 1)
    return rows == cols


def inverse_into(out_ref, matrix, least, most, short_steps):
    order = matrix.shape[0]
    unit = jnp.where(eye(order), 1.0, 0.0).astype(F32)
    high, low = split(matrix)
    floor = least / most
    scale = 2.0 / (most + least)
    estimate = scale * (2.0 * unit - scale * matrix)
    floor = 4.0 * floor / ((1.0 + floor) * (1.0 + floor))
    for _ in range(short_steps):
        scale = 2.0 / (1.0 + floor)
        short = estimate.astype(BF16)
        rest = unit - scale * dot1(high, short)
        estimate = scale * (short.astype(F32) + dot1(short, rest.astype(BF16)))
        floor = 4.0 * floor / ((1.0 + floor) * (1.0 + floor))
    short = estimate.astype(BF16)
    rest = unit - (dot1(high, short) + dot1(low, short))
    estimate = short.astype(F32) + dot1(short, rest.astype(BF16))
    est_high, est_low = split(estimate)
    rest = unit - (dot1(high, est_high) + (dot1(high, est_low) + dot1(low, est_high)))
    out_ref[...] = estimate + dot1(est_high, rest.astype(BF16))
    size = jnp.sum(rest * rest)

    @pl.when(jnp.logical_not(size < 1e-6))
    def _():
        first = 2.0 / (most + least)
        out_ref[...] = first * (2.0 * unit - first * matrix)

        def step(_, floor):
            scale = 2.0 / (1.0 + floor)
            current = out_ref[...]
            left = unit - scale * dot6(matrix, current)
            out_ref[...] = scale * (current + dot6(current, left))
            return 4.0 * floor / ((1.0 + floor) * (1.0 + floor))

        start = least / most
        start = 4.0 * start / ((1.0 + start) * (1.0 + start))
        lax.fori_loop(0, FALLBACK_STEPS, step, start)


def leaf_kernel(rank, d_ref, u_ref, g_ref, dinv_ref, yut_ref, w_ref, inv_ref):
    order = d_ref.shape[0]
    core = lax.axis_index("rows")
    block = d_ref[...]
    diag_row = jnp.sum(jnp.where(eye(order), block, 0.0), axis=0, keepdims=True)
    diag_col = jnp.sum(jnp.where(eye(order), block, 0.0), axis=1, keepdims=True)
    row_total = jnp.sum(jnp.abs(block), axis=1, keepdims=True)
    least = jnp.min((2.0 * diag_col - row_total) / diag_col, axis=0, keepdims=True)
    least = jnp.maximum(least, 2.0**-22)
    scale_row = lax.rsqrt(diag_row)
    scale_col = lax.rsqrt(diag_col)
    inverse_into(inv_ref, block * scale_row * scale_col, least, 2.0 - least, 5)
    inverse = inv_ref[...] * scale_row * scale_col
    dinv_ref[...] = inverse
    first = dot3(u_ref[:, :rank], g_ref[...])
    basis = jnp.concatenate([first, u_ref[:, rank:]], axis=1)
    solved = dot3(basis.T, inverse)
    yut_ref[...] = solved
    weight = dot3(solved, basis)
    part = lambda i, j: weight[i * rank : (i + 1) * rank, j * rank : (j + 1) * rank]
    w_ref[core] = jnp.concatenate([part(0, 0), part(0, 1), part(0, 2)], axis=0)
    w_ref[1 - core] = jnp.concatenate([part(1, 1), part(1, 2), part(2, 2)], axis=0)


def project_kernel(yut_ref, rhs_ref, p_ref):
    spot = lax.axis_index(AXES) % 4
    width = rhs_ref.shape[1] // 4
    solved = yut_ref[...]
    for chunk in range(4):
        start = pl.multiple_of((spot ^ chunk) * width, width)
        p_ref[chunk] = dot3(solved, rhs_ref[:, pl.ds(start, width)])


def solve_kernel(dinv_ref, rhs_ref, out_ref):
    out_ref[...] = dot3(dinv_ref[...], rhs_ref[...])


def refine(matrix, inverse, right):
    found = dot3(inverse, right)
    return found + dot1(inverse.astype(BF16), (right - dot3(matrix, found)).astype(BF16))


def lift_kernel_matrix(rank, count, mine_ref, other_ref, *refs):
    pieces, (half_ref, inv_ref, mat_ref, found_ref, link_ref, next_ref) = refs[:4], refs[4:]
    core = lax.axis_index("rows")
    spot = lax.axis_index(AXES) // (4 if count == 2 else 1) % 4
    mine, other = mine_ref[...], other_ref[...]
    both = jnp.concatenate(
        [jnp.where(core == 0, mine, other), jnp.where(core == 0, other, mine)], axis=0
    )
    part = lambda k: both[k * rank : (k + 1) * rank]
    unit = jnp.where(eye(rank), 1.0, 0.0).astype(F32)
    matrix = unit + part(0)
    most = jnp.max(jnp.sum(jnp.abs(matrix), axis=1, keepdims=True), axis=0, keepdims=True)
    inverse_into(inv_ref, matrix, jnp.ones_like(most), most, 4)
    mat_ref[...] = matrix
    links = [part(k) for k in range(1, count)]
    link = jnp.concatenate(links, axis=1)
    link_ref[...] = link
    found = refine(matrix, inv_ref[...], link)
    found_ref[...] = found
    height = pieces[0].shape[0]
    for chunk in range(4):
        start = pl.multiple_of((spot ^ chunk) * height, height)
        next_ref[pl.ds(start, height), :] = pieces[chunk][...]
    below = dot3(link.T, found)
    cell = lambda i, j: below[i * rank : (i + 1) * rank, j * rank : (j + 1) * rank]
    coupling = next_ref[...]
    turned = coupling.T
    if count == 3:
        top = dot3(dot3(turned, part(3) - cell(0, 0)), coupling)
        side = dot3(turned, part(4) - cell(0, 1))
        last = part(5) - cell(1, 1)
        whole = jnp.concatenate([top, side, last], axis=0)
        size = whole.shape[0] // 2
        half_ref[...] = jnp.where(core == 0, whole[:size], whole[size:])
    else:
        half_ref[...] = dot3(dot3(turned, part(2) - cell(0, 0)), coupling)


def lift_kernel_rhs(rank, p_ref, inv_ref, mat_ref, link_ref, next_ref, found_ref, up_ref):
    right = p_ref[...]
    found = refine(mat_ref[...], inv_ref[...], right[:rank])
    found_ref[...] = found
    rest = right[rank:] - dot3(link_ref[...].T, found)
    first = dot3(next_ref[...].T, rest[:rank])
    up_ref[:rank] = first
    if rest.shape[0] > rank:
        up_ref[rank:] = rest[rank:]


def top_kernel(rank, w_ref, p_ref, g1_ref, g2_ref, f0r_ref, f0_ref, f1r_ref, f1_ref, c_ref, inv_ref):
    unit = jnp.where(eye(rank), 1.0, 0.0).astype(F32)
    matrix = unit + w_ref[...]
    most = jnp.max(jnp.sum(jnp.abs(matrix), axis=1, keepdims=True), axis=0, keepdims=True)
    inverse_into(inv_ref, matrix, jnp.ones_like(most), most, 4)
    coeff_two = dot3(g2_ref[...], refine(matrix, inv_ref[...], p_ref[...]))
    coeff_one = dot3(g1_ref[...], f1r_ref[...] - dot3(f1_ref[...], coeff_two))
    lower = jnp.concatenate([coeff_one, coeff_two], axis=0)
    c_ref[:rank] = f0r_ref[...] - dot3(f0_ref[...], lower)
    c_ref[rank:] = lower


def finish_kernel(y_ref, yut_ref, c0_ref, c2_ref, c1_ref, out_ref):
    spot = lax.axis_index(AXES) % 4
    width = c0_ref.shape[1]
    solved = yut_ref[...].T
    coeffs = (c0_ref[...], c1_ref[0], c2_ref[...], c1_ref[1])
    for chunk in range(4):
        cols = pl.ds(pl.multiple_of((spot ^ chunk) * width, width), width)
        out_ref[:, cols] = y_ref[:, cols] - dot3(solved, coeffs[chunk])


def call(kernel, outs, scratch=(), name=None):
    return lambda *args: pl.pallas_call(
        kernel,
        out_shape=outs,
        in_specs=[VMEM] * len(args),
        out_specs=jax.tree.map(lambda _: VMEM, outs),
        scratch_shapes=list(scratch),
        name=name,
    )(*args)


def shape(*sizes):
    return jax.ShapeDtypeStruct(sizes, F32)


def per_device(diag_blocks, rhs, bases, coupling_one, coupling_two, coupling_top):
    rank = coupling_one.shape[1]
    order, rhs_cols = rhs.shape
    all_cols = bases.shape[1]
    width = rhs_cols // 4
    all_bits = lax.axis_size(AXES).bit_length() - 1

    two_rows = coupling_two.shape[0]
    packed = jnp.concatenate([coupling_two, coupling_top], axis=0)
    around = [packed] + [partner(packed, k) for k in (1, 2, 3)]
    one_pieces = [piece[:two_rows] for piece in around]

    dinv, solved_t, weights = call(
        functools.partial(leaf_kernel, rank),
        (shape(order, order), shape(all_cols, order), shape(2, 3 * rank, rank)),
        [pltpu.VMEM((order, order), F32)],
        "leaf",
    )(diag_blocks, bases, coupling_one)

    mine = weights[0] + partner(weights[1], 1)
    projected = call(project_kernel, shape(4, all_cols, width), name="project")(solved_t, rhs)
    mine = mine + partner(mine, 2)
    sent = jnp.stack([projected[1], projected[3]])
    got = partner(sent, 1)
    other = partner(mine, 1)
    solution_part = call(solve_kernel, shape(order, rhs_cols), name="solve")(dinv, rhs)
    right = projected[0] + got[0] + partner(projected[2] + got[1], 2)

    top_pieces = [piece[two_rows:] for piece in around]
    spot = lax.axis_index(AXES) % 4
    stacked = jnp.stack(top_pieces)
    ordered = jnp.concatenate([stacked[spot ^ k] for k in range(4)], axis=0)
    top_around = [ordered] + [partner(ordered, k) for k in (4, 8, 12)]

    half, inv0, mat0, found0, link0, coup1 = call(
        functools.partial(lift_kernel_matrix, rank, 3),
        (shape(3 * rank // 2, rank), shape(rank, rank), shape(rank, rank), shape(rank, 2 * rank), shape(rank, 2 * rank), shape(rank, rank)),
        name="lift_zero",
    )(mine, other, *one_pieces)
    half = half + partner(half, 4)
    found0r, right = call(
        functools.partial(lift_kernel_rhs, rank),
        (shape(rank, width), shape(2 * rank, width)),
        name="lift_zero_rhs",
    )(right, inv0, mat0, link0, coup1)
    half = half + partner(half, 8)
    right = right + partner(right, 4)
    other = partner(half, 1)
    right = right + partner(right, 8)

    last, inv1, mat1, found1, link1, coup2 = call(
        functools.partial(lift_kernel_matrix, rank, 2),
        (shape(rank, rank), shape(rank, rank), shape(rank, rank), shape(rank, rank), shape(rank, rank), shape(rank, rank)),
        name="lift_one",
    )(half, other, *top_around)
    found1r, right = call(
        functools.partial(lift_kernel_rhs, rank),
        (shape(rank, width), shape(rank, width)),
        name="lift_one_rhs",
    )(right, inv1, mat1, link1, coup2)
    for bit in range(4, all_bits):
        last = last + partner(last, 1 << bit)
        right = right + partner(right, 1 << bit)
    coeffs = call(
        functools.partial(top_kernel, rank),
        shape(all_cols, width),
        [pltpu.VMEM((rank, rank), F32)],
        "top",
    )(last, right, coup1, coup2, found0r, found0, found1r, found1)
    coeffs_x = partner(coeffs, 2)
    coeffs_core = partner(jnp.stack([coeffs, coeffs_x]), 1)
    return call(finish_kernel, shape(order, rhs_cols), name="finish")(
        solution_part, solved_t, coeffs, coeffs_x, coeffs_core
    )


def solution(mesh):
    placed = (P(AXES, None),) * 6
    return jax.shard_map(
        per_device, mesh=mesh, in_specs=placed, out_specs=P(AXES, None), check_vma=False
    )
```
